32 devices in a mesh: dp: 2 (over core), context: 4 (over z), tensor: 4 (over y, x).
Axes of the slice: x: 2, y: 2, z: 4, core: 2. Of those that a mesh axis runs over, the one named last changes fastest.
Arguments:
- block_in: float32 [2, 2048, 1024], P('dp', 'context'), may hold values from -6 to 6
- segments: int32 [2, 2048], P('dp', 'context'), may hold values from 0 to 3, never falling along the last dimension, each value on 1 to 1024 neighbouring positions
- cotangent: float32 [2, 2048, 1024], P('dp', 'context'), may hold values from -6 to 6
- norm_gain: bfloat16 [1024], P(('dp', 'context')), may hold values from 0.5 to 1.5
- w_query: bfloat16 [1024, 512], P(('dp', 'context'), 'tensor'), may hold values from -0.1875 to 0.1875
- w_key: bfloat16 [1024, 512], P(('dp', 'context'), 'tensor'), may hold values from -0.1875 to 0.1875
- w_value: bfloat16 [1024, 1024], P(('dp', 'context'), 'tensor'), may hold values from -0.1875 to 0.1875
- w_gate_out: bfloat16 [1024, 1024], P(('dp', 'context'), 'tensor'), may hold values from -0.1875 to 0.1875
- w_rank_in: bfloat16 [1024, 16], P(('dp', 'context')), may hold values from -0.1875 to 0.1875
- w_rank_out: float32 [512, 16], P('tensor'), may hold values from -1.5 to 1.5
- gate_bias: float32 [512], P('tensor'), may hold values from 0 to 13
- group_gain: float32 [256], replicated, may hold values from 0.5 to 1.5
- w_output: bfloat16 [1024, 1024], P(('dp', 'context'), 'tensor'), may hold values from -0.25 to 0.25
- mlp_gain: bfloat16 [1024], P(('dp', 'context')), may hold values from 0.5 to 1.5
- w_gate: bfloat16 [1024, 2816], P(('dp', 'context'), 'tensor'), may hold values from -0.1875 to 0.1875
- w_up: bfloat16 [1024, 2816], P(('dp', 'context'), 'tensor'), may hold values from -0.1875 to 0.1875
- w_down: bfloat16 [1024, 2816], P(('dp', 'context'), 'tensor'), may hold values from -0.15625 to 0.15625
Outputs:
- block_out: float32 [2, 2048, 1024], P('dp', 'context')
- d_block_in: float32 [2, 2048, 1024], P('dp', 'context')
- d_norm_gain: float32 [1024], P(('dp', 'context'))
- d_w_query: float32 [1024, 512], P(('dp', 'context'), 'tensor')
- d_w_key: float32 [1024, 512], P(('dp', 'context'), 'tensor')
- d_w_value: float32 [1024, 1024], P(('dp', 'context'), 'tensor')
- d_w_gate_out: float32 [1024, 1024], P(('dp', 'context'), 'tensor')
- d_w_rank_in: float32 [1024, 16], P(('dp', 'context'))
- d_w_rank_out: float32 [512, 16], P('tensor')
- d_gate_bias: float32 [512], P('tensor')
- d_group_gain: float32 [256], replicated
- d_w_output: float32 [1024, 1024], P(('dp', 'context'), 'tensor')
- d_mlp_gain: float32 [1024], P(('dp', 'context'))
- d_w_gate: float32 [1024, 2816], P(('dp', 'context'), 'tensor')
- d_w_up: float32 [1024, 2816], P(('dp', 'context'), 'tensor')
- d_w_down: float32 [1024, 2816], P(('dp', 'context'), 'tensor')
The draws below stay inside these ranges and needn't reach their ends.
Inputs may be any that keep to these rules, and one draw needn't show every extreme that they name: `segments`: along each sequence the segment numbers never fall; a document holds at most 1024 tokens and one holds exactly that many.
All inputs are finite; a program needn't handle non-finite values.
Results may differ from the reference program's by a relative error of at most 0.012.
Values may be sent and summed in bfloat16 or wider, within the bound.
A program may use at most 256 MiB of HBM per device.

```python
import math
import jax
import jax.numpy as jnp
import numpy as np
from jax import lax

D = 1024
HEADS = 4
HEAD_K = 128
HEAD_V = 256
RANK = 16
FF = 2816
BLOCK = 64
SEQS = 2
LEN = 2048
KEYS = 512
VALS = 1024


def block_levels(key, extent, split, least, top_value):
    gain, own = 1.0, jax.random.fold_in(key, 6)
    for dim, parts in split:
        heights = jnp.exp(jax.random.uniform(jax.random.fold_in(own, dim), (parts,), jnp.float32, least / len(split), top_value / len(split)))
        gain = gain * jnp.repeat(heights, extent[dim] // parts).reshape([-1 if axis == dim else 1 for axis in range(len(extent))])
    return gain


def split_up(amount, total, limit, slope):
    weights = [(1 << 20) // math.isqrt(grade ** slope) + 1 for grade in range(2, amount + 1)]
    rest, given = total - limit - (amount - 1), [1] * (amount - 1)
    while rest > 0:
        free = [i for i in range(amount - 1) if given[i] < limit]
        pool, remaining = sum([weights[i] for i in free]), rest
        for i in free:
            extra = min(limit - given[i], max(1, remaining * weights[i] // pool), rest)
            given[i] = given[i] + extra
            rest = rest - extra
    return np.array([limit] + given)


def uneven(own_key, count, total, bound, slope):
    if count == 2:
        one = jax.random.randint(own_key, (), max(1, total - bound), min(bound, total - 1) + 1)
        return jnp.stack([one, total - one])
    tallies = jnp.asarray(split_up(count, total, bound, slope), jnp.int32)
    pairs = (count - 1) // 2
    source_of, taker = tallies[1:1 + 2 * pairs:2], tallies[2:2 + 2 * pairs:2]
    margin = jnp.minimum(source_of - 1, bound - taker)
    moved = jax.random.randint(jax.random.fold_in(own_key, 1), (pairs,), 0, 1 << 20) % (margin + 1)
    tallies = tallies.at[1:1 + 2 * pairs:2].set(source_of - moved).at[2:2 + 2 * pairs:2].set(taker + moved)
    return tallies[jax.random.permutation(jax.random.fold_in(own_key, 2), count)]


def bell_draw(own_key, shape, scale, bound, cuts=(), kind=jnp.bfloat16):
    loudness = block_levels(own_key, shape, cuts, -0.22, 0.18) if cuts else 1.0
    drawn = jax.random.normal(own_key, shape, jnp.float32) * scale * loudness
    return jnp.minimum(jnp.maximum(drawn, -bound), bound).astype(kind)


def setup_inputs(seed: int = 0) -> dict:
    key_list = jax.random.split(jax.random.key(seed), 18)
    return {
        "block_in": bell_draw(key_list[0], (SEQS, LEN, D), 1.0, 6.0, ((0, 2), (1, 4)), jnp.float32),
        "segments": jax.vmap(lambda own: jnp.searchsorted(jnp.cumsum(uneven(own, 4, LEN, LEN // 2, 0)), jnp.arange(LEN), side="right"))(jax.random.split(key_list[1], SEQS)).reshape((SEQS, LEN)).astype(jnp.int32),
        "cotangent": bell_draw(key_list[2], (SEQS, LEN, D), 1.0, 6.0, ((0, 2), (1, 4)), jnp.float32),
        "norm_gain": jnp.clip(1.0 + 0.1 * jax.random.normal(key_list[3], (D,), jnp.float32), 0.5, 1.5).astype(jnp.bfloat16),
        "w_query": bell_draw(key_list[4], (D, KEYS), D ** -0.5, 0.1875, ((0, 8), (1, 4))),
        "w_key": bell_draw(key_list[5], (D, KEYS), D ** -0.5, 0.1875, ((0, 8), (1, 4))),
        "w_value": bell_draw(key_list[6], (D, VALS), D ** -0.5, 0.1875, ((0, 8), (1, 4))),
        "w_gate_out": bell_draw(key_list[7], (D, VALS), D ** -0.5, 0.1875, ((0, 8), (1, 4))),
        "w_rank_in": bell_draw(key_list[8], (D, RANK), D ** -0.5, 0.1875, ((0, 8),)),
        "w_rank_out": bell_draw(key_list[9], (KEYS, RANK), RANK ** -0.5, 1.5, ((0, 4),), jnp.float32),
        "gate_bias": jnp.clip(13.0 * jax.random.uniform(key_list[10], (KEYS,), jnp.float32) ** block_levels(key_list[10], (KEYS,), ((0, 4),), -0.2, 0.2), 0.0, 13.0),
        "group_gain": jnp.clip(1.0 + 0.1 * jax.random.normal(key_list[11], (HEAD_V,), jnp.float32), 0.5, 1.5),
        "w_output": bell_draw(key_list[12], (D, VALS), (VALS // 2) ** -0.5, 0.25, ((0, 8), (1, 4))),
        "mlp_gain": jnp.clip(1.0 + 0.1 * jax.random.normal(key_list[13], (D,), jnp.float32), 0.5, 1.5).astype(jnp.bfloat16),
        "w_gate": bell_draw(key_list[14], (D, FF), D ** -0.5, 0.1875, ((0, 8), (1, 4))),
        "w_up": bell_draw(key_list[15], (D, FF), D ** -0.5, 0.1875, ((0, 8), (1, 4))),
        "w_down": bell_draw(key_list[16], (D, FF), (FF // 2) ** -0.5, 0.15625, ((0, 8), (1, 4))),
    }


epsilon = 1e-06
gate_divisor = 16.0
highest_precision = lax.Precision.HIGHEST

def block_step(carried_in, pieces):
    carried_over, seg_prev = carried_in
    query_rows, key_vecs, value_vectors, decay_log, seg_block = pieces
    running_total = jnp.cumsum(decay_log, axis=0)
    length = query_rows.shape[0]
    causal = jnp.arange(length)[:, None] >= jnp.arange(length)[None, :]
    allowed = (causal & (seg_block[:, None] == seg_block[None, :]))[:, :, None, None]
    spread = running_total[:, None] - running_total[None, :]
    factor = jnp.where(allowed, jnp.exp(jnp.where(allowed, spread, 0.0)), 0.0)
    scores = jnp.einsum('thk,shk,tshk->tsh', query_rows, key_vecs, factor, precision=highest_precision)
    output_rows = jnp.einsum('tsh,shv->thv', scores, value_vectors, precision=highest_precision)
    state_reading = (seg_block == seg_prev).astype(jnp.float32)[:, None, None]
    output_rows = output_rows + state_reading * jnp.einsum('qou,ouj->qoj', query_rows * jnp.exp(running_total), carried_over, precision=highest_precision)
    last_seg = seg_block[-1]
    in_tail = (seg_block == last_seg).astype(jnp.float32)[:, None, None]
    weighted_sum = key_vecs * jnp.exp(running_total[-1][None] - running_total) * in_tail
    keep_factor = (seg_prev == last_seg).astype(jnp.float32)
    carried_over = jnp.einsum('mzp,mzx->zpx', weighted_sum, value_vectors, precision=highest_precision) + keep_factor * jnp.exp(running_total[-1])[:, :, None] * carried_over
    return ((carried_over, last_seg), output_rows)

def linear_attention(query_rows, key_vecs, value_vectors, decay_log, seg_row):
    blocks = query_rows.shape[0] // BLOCK

    def to_blocks(values_in):
        return values_in.reshape((blocks, BLOCK) + values_in.shape[1:])
    initial = (jnp.zeros((query_rows.shape[1], query_rows.shape[2], value_vectors.shape[2]), jnp.float32), jnp.int32(-1))
    _, output_rows = lax.scan(jax.checkpoint(block_step), initial, (to_blocks(query_rows), to_blocks(key_vecs), to_blocks(value_vectors), to_blocks(decay_log), to_blocks(seg_row)))
    return output_rows.reshape(query_rows.shape[0], query_rows.shape[1], value_vectors.shape[2])

def gated_norm(mixed_core, out_gate, group_gain):
    inverse_rms = lax.rsqrt(lax.optimization_barrier(jnp.mean(mixed_core * mixed_core, axis=-1, keepdims=True)) + epsilon)
    return mixed_core * inverse_rms * group_gain * jax.nn.silu(out_gate)

def decay_map(rank_act, w_rank_out, gate_bias):
    return jax.nn.log_sigmoid(jnp.dot(rank_act, w_rank_out.T, precision=highest_precision) + gate_bias) / gate_divisor

def norm_back(scaled_grad, unit_rows, rstd_rows):
    return rstd_rows * (scaled_grad - unit_rows * lax.optimization_barrier(jnp.mean(scaled_grad * unit_rows, axis=-1, keepdims=True)))

def reference(block_in, segments, cotangent, norm_gain, w_query, w_key, w_value, w_gate_out, w_rank_in, w_rank_out, gate_bias, group_gain, w_output, mlp_gain, w_gate, w_up, w_down):
    query_scale = HEAD_K ** (-0.5)
    gain_one = norm_gain.astype(jnp.float32)
    gain_two = mlp_gain.astype(jnp.float32)

    def one_sequence(inputs):
        hidden_in, seg_row, grad_out = inputs
        tokens = hidden_in.shape[0]
        rstd_one = lax.rsqrt(lax.optimization_barrier(jnp.mean(hidden_in * hidden_in, axis=-1, keepdims=True)) + epsilon)
        unit_one = hidden_in * rstd_one
        normed_one = (unit_one * gain_one).astype(jnp.bfloat16)
        query_rows = jnp.dot(normed_one, w_query, preferred_element_type=jnp.float32) * query_scale
        key_vecs = jnp.dot(normed_one, w_key, preferred_element_type=jnp.float32)
        value_vectors = jnp.dot(normed_one, w_value, preferred_element_type=jnp.float32)
        out_gate = jnp.dot(normed_one, w_gate_out, preferred_element_type=jnp.float32)
        rank_act = jnp.dot(normed_one, w_rank_in, preferred_element_type=jnp.float32)
        decay_log, decay_pull = jax.vjp(decay_map, rank_act, w_rank_out, gate_bias)

        def attend(query_part, key_part, value_part, decay_part):
            return linear_attention(query_part, key_part, value_part, decay_part, seg_row)
        mixed_core, attend_pull = jax.vjp(attend, query_rows.reshape(tokens, HEADS, HEAD_K), key_vecs.reshape(tokens, HEADS, HEAD_K), value_vectors.reshape(tokens, HEADS, HEAD_V), decay_log.reshape(tokens, HEADS, HEAD_K))
        gated_full, gate_pull = jax.vjp(gated_norm, mixed_core, out_gate.reshape(tokens, HEADS, HEAD_V), group_gain)
        gated_out = gated_full.reshape(tokens, VALS).astype(jnp.bfloat16)
        residual = hidden_in + jnp.dot(gated_out, w_output.T, preferred_element_type=jnp.float32)
        rstd_two = lax.rsqrt(lax.optimization_barrier(jnp.mean(residual * residual, axis=-1, keepdims=True)) + epsilon)
        unit_two = residual * rstd_two
        normed_two = (unit_two * gain_two).astype(jnp.bfloat16)
        gate_pre = jnp.dot(normed_two, w_gate, preferred_element_type=jnp.float32)
        up_value = jnp.dot(normed_two, w_up, preferred_element_type=jnp.float32)
        sigmoid_gate = jax.nn.sigmoid(gate_pre)
        activation = (gate_pre * sigmoid_gate * up_value).astype(jnp.bfloat16)
        block_out = residual + jnp.dot(activation, w_down.T, preferred_element_type=jnp.float32)
        grad_low = grad_out.astype(jnp.bfloat16)
        d_activation = jnp.dot(grad_low, w_down, preferred_element_type=jnp.float32)
        d_w_down = jnp.dot(grad_low.T, activation, preferred_element_type=jnp.float32)
        d_gate_pre = (d_activation * up_value * sigmoid_gate * (1.0 + gate_pre * (1.0 - sigmoid_gate))).astype(jnp.bfloat16)
        d_up_value = (d_activation * gate_pre * sigmoid_gate).astype(jnp.bfloat16)
        d_w_gate = jnp.dot(normed_two.T, d_gate_pre, preferred_element_type=jnp.float32)
        d_w_up = jnp.dot(normed_two.T, d_up_value, preferred_element_type=jnp.float32)
        dnormed_two = jnp.dot(d_gate_pre, w_gate.T, preferred_element_type=jnp.float32) + jnp.dot(d_up_value, w_up.T, preferred_element_type=jnp.float32)
        d_mlp_gain = lax.optimization_barrier(jnp.sum(dnormed_two * unit_two, axis=0))
        d_residual = grad_out + norm_back(dnormed_two * gain_two, unit_two, rstd_two)
        residual_low = d_residual.astype(jnp.bfloat16)
        d_gated_out = jnp.dot(residual_low, w_output, preferred_element_type=jnp.float32)
        d_w_output = jnp.dot(residual_low.T, gated_out, preferred_element_type=jnp.float32)
        mixed_core_gradient, d_out_gate, d_group_gain = gate_pull(d_gated_out.reshape(tokens, HEADS, HEAD_V))
        d_queries, d_key_vecs, d_val_vecs, d_decay_log = attend_pull(mixed_core_gradient)
        d_rank_act, d_w_rank_out, d_gate_bias = decay_pull(d_decay_log.reshape(tokens, KEYS))
        query_low = (d_queries.reshape(tokens, KEYS) * query_scale).astype(jnp.bfloat16)
        key_low = d_key_vecs.reshape(tokens, KEYS).astype(jnp.bfloat16)
        value_low = d_val_vecs.reshape(tokens, VALS).astype(jnp.bfloat16)
        gate_low = d_out_gate.reshape(tokens, VALS).astype(jnp.bfloat16)
        rank_low = d_rank_act.astype(jnp.bfloat16)
        d_w_query = jnp.dot(normed_one.T, query_low, preferred_element_type=jnp.float32)
        d_w_key = jnp.dot(normed_one.T, key_low, preferred_element_type=jnp.float32)
        d_w_value = jnp.dot(normed_one.T, value_low, preferred_element_type=jnp.float32)
        d_w_gate_out = jnp.dot(normed_one.T, gate_low, preferred_element_type=jnp.float32)
        d_w_rank_in = jnp.dot(normed_one.T, rank_low, preferred_element_type=jnp.float32)
        dnormed_one = jnp.dot(query_low, w_query.T, preferred_element_type=jnp.float32) + jnp.dot(key_low, w_key.T, preferred_element_type=jnp.float32) + jnp.dot(value_low, w_value.T, preferred_element_type=jnp.float32) + jnp.dot(gate_low, w_gate_out.T, preferred_element_type=jnp.float32) + jnp.dot(rank_low, w_rank_in.T, preferred_element_type=jnp.float32)
        d_norm_gain = lax.optimization_barrier(jnp.sum(dnormed_one * unit_one, axis=0))
        d_block_in = d_residual + norm_back(dnormed_one * gain_one, unit_one, rstd_one)
        return (block_out, d_block_in, d_norm_gain, d_w_query, d_w_key, d_w_value, d_w_gate_out, d_w_rank_in, d_w_rank_out, d_gate_bias, d_group_gain, d_w_output, d_mlp_gain, d_w_gate, d_w_up, d_w_down)
    results = lax.map(one_sequence, (block_in, segments, cotangent))
    summed = [lax.optimization_barrier(jnp.sum(item, axis=0)) for item in results[2:]]
    return (results[0], results[1], summed[0], summed[1], summed[2], summed[3], summed[4], summed[5], summed[6], summed[7], summed[8], summed[9], summed[10], summed[11], summed[12], summed[13])
```

```python
import functools

import jax
import jax.numpy as jnp
from jax import lax
from jax.experimental import pallas as pl
from jax.experimental.pallas import tpu as pltpu
from jax.sharding import PartitionSpec as P

HEAD_K = 128
HEAD_V = 256
TILE = 256

epsilon = 1e-06
gate_divisor = 16.0
highest_precision = lax.Precision.HIGHEST
low = jnp.bfloat16
f32 = jnp.float32
VMEM = pl.BlockSpec(memory_space=pltpu.VMEM)


def mm(a, b, ca=1, cb=0):
    return lax.dot_general(
        a.astype(low), b.astype(low), (((ca,), (cb,)), ((), ())), preferred_element_type=f32
    )


def mm_full(a, b, ca=1, cb=0):
    return lax.dot_general(
        a, b, (((ca,), (cb,)), ((), ())), precision=highest_precision, preferred_element_type=f32
    )


def mask_sum(mask, values):
    hi = values.astype(low)
    rest = values - hi.astype(f32)
    mid = rest.astype(low)
    last = (rest - mid.astype(f32)).astype(low)
    return mm(mask, hi) + mm(mask, mid) + mm(mask, last)


def level_factor(total, half):
    rows, width = total.shape
    if 2 * half >= 16:
        cube = total.reshape(rows // (2 * half), 2 * half, width)
        diff = cube - cube[:, half - 1 : half, :]
    else:
        cube = total.reshape(rows // 8, 8, width)
        sub = lax.broadcasted_iota(jnp.int32, cube.shape, 1)
        mid = cube[:, half - 1 : half, :]
        for block in range(1, 8 // (2 * half)):
            at = block * 2 * half
            mid = jnp.where(sub >= at, cube[:, at + half - 1 : at + half, :], mid)
        diff = cube - mid
    return jnp.exp(jnp.minimum(diff, -diff)).reshape(rows, width)


def small_levels(tile):
    half = tile // 2
    out = []
    while half >= 1:
        out.append(half)
        half //= 2
    return out


def level_mask(half, tile):
    t = lax.broadcasted_iota(jnp.int32, (tile, tile), 0)
    s = lax.broadcasted_iota(jnp.int32, (tile, tile), 1)
    return (t // (2 * half) == s // (2 * half)) & (t % (2 * half) >= half) & (s % (2 * half) < half)


def large_levels(rows, tile):
    half = rows // 2
    out = []
    while half >= tile:
        out.append(half)
        half //= 2
    return out


def local_kernel(heads, proj, rank_out, bias, seg_col, seg_row, out_ref, state_ref, lifted_ref, total_ref, tail_ref):
    rows = proj.shape[0]
    tile = min(TILE, rows)
    kw, vw = heads * HEAD_K, heads * HEAD_V
    rank = rank_out.shape[1]
    rank_act = proj[:, 2 * kw + 2 * vw : 2 * kw + 2 * vw + rank]
    decay = jax.nn.log_sigmoid(mm_full(rank_act, rank_out[...], 1, 1) + bias[...]) / gate_divisor
    segc, segr = seg_col[...], seg_row[...]
    t = lax.broadcasted_iota(jnp.int32, (rows, rows), 0)
    s = lax.broadcasted_iota(jnp.int32, (rows, rows), 1)
    total = mask_sum((t >= s).astype(low), decay)
    total_ref[...] = total
    same = segc == segr
    tail = (segc == segr[:, rows - 1 : rows]).astype(f32)
    for h in range(heads):
        q = proj[:, h * HEAD_K : (h + 1) * HEAD_K] * HEAD_K**-0.5
        k = proj[:, kw + h * HEAD_K : kw + (h + 1) * HEAD_K]
        v = proj[:, 2 * kw + h * HEAD_V : 2 * kw + (h + 1) * HEAD_V].astype(low)
        g = total[:, h * HEAD_K : (h + 1) * HEAD_K]
        diag = jnp.sum(q * k, axis=1, keepdims=True)
        ti = lax.broadcasted_iota(jnp.int32, (tile, tile), 0)
        si = lax.broadcasted_iota(jnp.int32, (tile, tile), 1)
        tiles = rows // tile
        sums = [
            jnp.where(ti == si, diag[i * tile : (i + 1) * tile], 0.0) for i in range(tiles)
        ]
        for half in small_levels(tile):
            factor = level_factor(g, half)
            qh, kh = (q * factor).astype(low), (k * factor).astype(low)
            mask = level_mask(half, tile)
            for i in range(tiles):
                span = slice(i * tile, (i + 1) * tile)
                sums[i] = jnp.where(mask, mm(qh[span], kh[span], 1, 1), sums[i])
        outs = []
        for i in range(tiles):
            span = slice(i * tile, (i + 1) * tile)
            sc = jnp.where(same[span, span] & (ti >= si), sums[i], 0.0)
            outs.append(mm(sc, v[span]))
        for half in large_levels(rows, tile):
            factor = level_factor(g, half)
            qh, kh = (q * factor).astype(low), (k * factor).astype(low)
            for at in range(0, rows, 2 * half):
                right, left = slice(at + half, at + 2 * half), slice(at, at + half)
                sc = jnp.where(same[right, left], mm(qh[right], kh[left], 1, 1), 0.0)
                more = mm(sc, v[left])
                for i in range(half // tile):
                    outs[(at + half) // tile + i] += more[i * tile : (i + 1) * tile]
        for i in range(tiles):
            out_ref[i * tile : (i + 1) * tile, h * HEAD_V : (h + 1) * HEAD_V] = outs[i]
        end = g[rows - 1 : rows]
        kt = k * jnp.exp(end - g) * tail
        state_ref[h] = mm(kt, v, 0, 0)
        lifted_ref[:, h * HEAD_K : (h + 1) * HEAD_K] = (q * jnp.exp(g)).astype(low)
        tail_ref[:, h * HEAD_K : (h + 1) * HEAD_K] = jnp.exp(end)


def intra_back_kernel(heads, proj, total_in, d_mixed, seg_col, seg_row, dq_ref, dk_ref, dv_ref, dg_ref):
    rows = proj.shape[0]
    tile = min(TILE, rows)
    tiles = rows // tile
    kw = heads * HEAD_K
    same = seg_col[...] == seg_row[...]
    ti = lax.broadcasted_iota(jnp.int32, (tile, tile), 0)
    si = lax.broadcasted_iota(jnp.int32, (tile, tile), 1)
    for h in range(heads):
        cols = slice(h * HEAD_K, (h + 1) * HEAD_K)
        vcols = slice(h * HEAD_V, (h + 1) * HEAD_V)
        q = proj[:, cols] * HEAD_K**-0.5
        k = proj[:, kw + h * HEAD_K : kw + (h + 1) * HEAD_K]
        v = proj[:, 2 * kw + h * HEAD_V : 2 * kw + (h + 1) * HEAD_V].astype(low)
        do = d_mixed[:, vcols].astype(low)
        g = total_in[:, cols]
        diag = jnp.sum(q * k, axis=1, keepdims=True)
        d_diag = jnp.sum(do.astype(f32) * v.astype(f32), axis=1, keepdims=True)
        sums = [jnp.where(ti == si, diag[i * tile : (i + 1) * tile], 0.0) for i in range(tiles)]
        allowed = [same[i * tile : (i + 1) * tile, i * tile : (i + 1) * tile] for i in range(tiles)]
        ds = [
            jnp.where(
                allowed[i],
                mm(do[i * tile : (i + 1) * tile], v[i * tile : (i + 1) * tile], 1, 1),
                0.0,
            ).astype(low)
            for i in range(tiles)
        ]
        dq = [(d_diag * k)[i * tile : (i + 1) * tile] for i in range(tiles)]
        dk = [(d_diag * q)[i * tile : (i + 1) * tile] for i in range(tiles)]
        dg = [jnp.zeros((tile, HEAD_K), f32) for i in range(tiles)]
        for half in small_levels(tile):
            factor = level_factor(g, half)
            qh, kh = (q * factor).astype(low), (k * factor).astype(low)
            mask = level_mask(half, tile)
            for i in range(tiles):
                span = slice(i * tile, (i + 1) * tile)
                sums[i] = jnp.where(mask, mm(qh[span], kh[span], 1, 1), sums[i])
                part = jnp.where(mask, ds[i], jnp.zeros((), low))
                dql = mm(part, kh[span])
                dkl = mm(part, qh[span], 0, 0)
                dq[i] += dql * factor[span]
                dk[i] += dkl * factor[span]
                dg[i] += qh[span].astype(f32) * dql - kh[span].astype(f32) * dkl
        dv = []
        for i in range(tiles):
            span = slice(i * tile, (i + 1) * tile)
            sc = jnp.where(allowed[i] & (ti >= si), sums[i], 0.0)
            dv.append(mm(sc, do[span], 0, 0))
        for half in large_levels(rows, tile):
            factor = level_factor(g, half)
            qh, kh = (q * factor).astype(low), (k * factor).astype(low)
            for at in range(0, rows, 2 * half):
                right, left = slice(at + half, at + 2 * half), slice(at, at + half)
                ok = same[right, left]
                sc = jnp.where(ok, mm(qh[right], kh[left], 1, 1), 0.0)
                part = jnp.where(ok, mm(do[right], v[left], 1, 1), 0.0).astype(low)
                dvl = mm(sc, do[right], 0, 0)
                dql = mm(part, kh[left])
                dkl = mm(part, qh[right], 0, 0)
                dgr = qh[right].astype(f32) * dql
                dgl = kh[left].astype(f32) * dkl
                dql = dql * factor[right]
                dkl = dkl * factor[left]
                for i in range(half // tile):
                    piece = slice(i * tile, (i + 1) * tile)
                    r, l = (at + half) // tile + i, at // tile + i
                    dq[r] += dql[piece]
                    dg[r] += dgr[piece]
                    dk[l] += dkl[piece]
                    dg[l] -= dgl[piece]
                    dv[l] += dvl[piece]
        for i in range(tiles):
            span = slice(i * tile, (i + 1) * tile)
            dq_ref[span, cols] = dq[i]
            dk_ref[span, cols] = dk[i]
            dg_ref[span, cols] = dg[i]
            dv_ref[span, vcols] = dv[i]


def silu_parts(gate):
    sig = jax.nn.sigmoid(gate)
    return sig, gate * sig


def mix_kernel(heads, proj, out_local, lifted, reading, prior, gain, mixed_ref, gated_ref):
    kw, vw = heads * HEAD_K, heads * HEAD_V
    for h in range(heads):
        vcols = slice(h * HEAD_V, (h + 1) * HEAD_V)
        mixed = out_local[:, vcols] + reading[...] * mm(
            lifted[:, h * HEAD_K : (h + 1) * HEAD_K], prior[h]
        )
        mixed_ref[:, vcols] = mixed
        rms = lax.rsqrt(jnp.mean(mixed * mixed, axis=1, keepdims=True) + epsilon)
        gate = proj[:, 2 * kw + vw + h * HEAD_V : 2 * kw + vw + (h + 1) * HEAD_V]
        gated_ref[:, vcols] = (mixed * rms * gain[...] * silu_parts(gate)[1]).astype(low)


def gate_back_kernel(heads, proj, mixed_in, d_gated_in, lifted, reading, gain, d_mixed_ref, gate_low_ref, gain_ref, direct_ref):
    kw, vw = heads * HEAD_K, heads * HEAD_V
    gain_sum = jnp.zeros((1, HEAD_V), f32)
    for h in range(heads):
        vcols = slice(h * HEAD_V, (h + 1) * HEAD_V)
        mixed = mixed_in[:, vcols]
        dy = d_gated_in[:, vcols]
        gate = proj[:, 2 * kw + vw + h * HEAD_V : 2 * kw + vw + (h + 1) * HEAD_V]
        sig, act = silu_parts(gate)
        rms = lax.rsqrt(jnp.mean(mixed * mixed, axis=1, keepdims=True) + epsilon)
        unit = mixed * rms
        gate_low_ref[:, vcols] = (
            dy * unit * gain[...] * sig * (1.0 + gate * (1.0 - sig))
        ).astype(low)
        gain_sum += jnp.sum(dy * act * unit, axis=0, keepdims=True)
        e = dy * act * gain[...]
        d_mixed = rms * (e - unit * jnp.mean(e * unit, axis=1, keepdims=True))
        d_mixed = d_mixed.astype(low)
        d_mixed_ref[:, vcols] = d_mixed
        read = lifted[:, h * HEAD_K : (h + 1) * HEAD_K] * reading[...].astype(low)
        direct_ref[h] = mm(read, d_mixed, 0, 0)
    gain_ref[...] = gain_sum


def finish_kernel(heads, rank, proj, total_in, d_mixed, lifted, reading, prior, later, through, rank_out, bias, gate_low, dq_in, dk_in, dv_in, dg_in, seg_col, seg_row, low_ref, rank_out_ref, bias_ref):
    rows = proj.shape[0]
    kw, vw = heads * HEAD_K, heads * HEAD_V
    segc, segr = seg_col[...], seg_row[...]
    t = lax.broadcasted_iota(jnp.int32, (rows, rows), 0)
    s = lax.broadcasted_iota(jnp.int32, (rows, rows), 1)
    suffix = ((t <= s) & (segc == segr)).astype(low)
    tail = (segc == segr[:, rows - 1 : rows]).astype(f32)
    read = reading[...]
    base = 2 * kw + 2 * vw
    rank_act = proj[:, base : base + rank]
    pre = mm_full(rank_act, rank_out[...], 1, 1) + bias[...]
    rank_part = jnp.zeros((rows, rank), f32)
    for h in range(heads):
        cols = slice(h * HEAD_K, (h + 1) * HEAD_K)
        vcols = slice(h * HEAD_V, (h + 1) * HEAD_V)
        k = proj[:, kw + h * HEAD_K : kw + (h + 1) * HEAD_K]
        v = proj[:, 2 * kw + h * HEAD_V : 2 * kw + (h + 1) * HEAD_V].astype(low)
        do = d_mixed[:, vcols]
        g = total_in[:, cols]
        end = g[rows - 1 : rows]
        pulled = mm(do, prior[h], 1, 1) * read
        dq = dq_in[:, cols] + pulled * jnp.exp(g)
        fall = jnp.exp(end - g) * tail
        kt = (k * fall).astype(low)
        dkt = mm(v, later[h], 1, 1)
        dk = dk_in[:, cols] + dkt * fall
        crossing = kt.astype(f32) * dkt
        dv = dv_in[:, vcols] + mm(kt, later[h])
        dg = dg_in[:, cols] + pulled * lifted[:, cols].astype(f32) - crossing
        across = jnp.sum(crossing, axis=0, keepdims=True) + through[:, cols]
        d_decay = mask_sum(suffix, dg) + tail * across
        d_pre = d_decay * jax.nn.sigmoid(-pre[:, cols]) / gate_divisor
        low_ref[:, cols] = (dq * HEAD_K**-0.5).astype(low)
        low_ref[:, kw + h * HEAD_K : kw + (h + 1) * HEAD_K] = dk.astype(low)
        low_ref[:, 2 * kw + h * HEAD_V : 2 * kw + (h + 1) * HEAD_V] = dv.astype(low)
        rank_part += mm_full(d_pre, rank_out[cols, :])
        rank_out_ref[cols, :] = mm_full(d_pre, rank_act, 0, 0)
        bias_ref[:, cols] = jnp.sum(d_pre, axis=0, keepdims=True)
    low_ref[:, 2 * kw + vw : base] = gate_low[...]
    wide = low_ref.shape[1] - base
    low_ref[:, base:] = jnp.concatenate(
        [rank_part, jnp.zeros((rows, wide - rank), f32)], axis=1
    ).astype(low)


def call(kernel, outs, *args):
    return pl.pallas_call(
        kernel,
        out_shape=[jax.ShapeDtypeStruct(shape, kind) for shape, kind in outs],
        in_specs=[VMEM] * len(args),
        out_specs=[VMEM] * len(outs),
        compiler_params=pltpu.CompilerParams(vmem_limit_bytes=56 * 1024 * 1024),
    )(*args)


def norm_back(scaled_grad, unit_rows, rstd_rows):
    return rstd_rows * (
        scaled_grad - unit_rows * jnp.mean(scaled_grad * unit_rows, axis=-1, keepdims=True)
    )


def gather(value):
    return lax.all_gather(value, ("dp", "context"), axis=0, tiled=True)


def scatter(value):
    return lax.psum_scatter(value, ("dp", "context"), scatter_dimension=0, tiled=True)


def dot32(a, b, ca=1, cb=0):
    return lax.dot_general(a, b, (((ca,), (cb,)), ((), ())), preferred_element_type=f32)


def chain(factors, values):
    weight = jnp.ones_like(factors[0])
    out = jnp.zeros_like(values[0])
    for j in reversed(range(factors.shape[0])):
        out = out + weight[..., None] * values[j]
        weight = weight * factors[j]
    return out


def per_device(
    block_in, segments, cotangent, norm_gain, w_query, w_key, w_value, w_gate_out, w_rank_in,
    w_rank_out, gate_bias, group_gain, w_output, mlp_gain, w_gate, w_up, w_down,
):
    hidden_in, seg, grad_out = block_in[0], segments[0], cotangent[0]
    tokens, width = hidden_in.shape
    rank = w_rank_in.shape[1]
    heads = w_rank_out.shape[0] // HEAD_K
    kw, vw = heads * HEAD_K, heads * HEAD_V
    base = 2 * kw + 2 * vw
    rest = -(rank + 2) % 128 + rank + 2
    rows_here = w_query.shape[0]
    seg_col, seg_row = seg[:, None], seg[None, :]
    bias = gate_bias[None, :]
    gain_g = group_gain[None, :]

    packed = jnp.concatenate(
        [
            w_query, w_key, w_value, w_gate_out, w_rank_in, norm_gain[:, None], mlp_gain[:, None],
            jnp.zeros((rows_here, rest - rank - 2), low), w_output,
        ],
        axis=1,
    )
    mixer = gather(packed)
    gate_w, up_w, down_w = gather(w_gate), gather(w_up), gather(w_down)
    wide = base + rest
    w_in = mixer[:, :wide]
    w_out = mixer[:, wide:]
    gain_one = mixer[:, base + rank].astype(f32)
    gain_two = mixer[:, base + rank + 1].astype(f32)

    rstd_one = lax.rsqrt(jnp.mean(hidden_in * hidden_in, axis=-1, keepdims=True) + epsilon)
    unit_one = hidden_in * rstd_one
    normed_one = (unit_one * gain_one).astype(low)
    proj = dot32(normed_one, w_in)
    out_local, state_local, lifted, total, ends = call(
        functools.partial(local_kernel, heads),
        [
            ((tokens, vw), f32), ((heads, HEAD_K, HEAD_V), f32), ((tokens, kw), low),
            ((tokens, kw), f32), ((1, kw), f32),
        ],
        proj, w_rank_out, bias, seg_col, seg_row,
    )
    peers, here = lax.axis_size("context"), lax.axis_index("context")
    firsts = lax.all_gather(jnp.stack([seg[0], seg[-1]]).astype(f32), "context")
    states = lax.all_gather(
        jnp.concatenate(
            [
                state_local.reshape(kw, HEAD_V),
                jnp.broadcast_to(ends.reshape(kw, 1), (kw, 128)),
            ],
            axis=1,
        ),
        "context",
    )
    order = jnp.arange(peers)
    first, last = firsts[:, 0], firsts[:, 1]
    before = jnp.concatenate([jnp.full((1,), -1.0, f32), last[:-1]])
    keep = jnp.where((first == before) | (before < 0.0), 1.0, 0.0)
    unbroken = jnp.where(first == last, 1.0, 0.0)
    decays = states[:, :, HEAD_V].reshape(peers, heads, HEAD_K)
    spans = decays * unbroken[:, None, None]
    passing = spans * keep[:, None, None]
    earlier = (order < here)[:, None, None]
    prior = chain(
        jnp.where(earlier, passing, 1.0),
        jnp.where(earlier[..., None], states[:, :, :HEAD_V].reshape(peers, heads, HEAD_K, HEAD_V), 0.0),
    )
    prior_last = jnp.where(here > 0, before[here], -1.0)
    reading = (seg.astype(f32) == prior_last).astype(f32)[:, None]

    mixed, gated = call(
        functools.partial(mix_kernel, heads),
        [((tokens, vw), f32), ((tokens, vw), low)],
        proj, out_local, lifted, reading, prior, gain_g,
    )
    attn = lax.psum(dot32(gated, w_out, 1, 1).astype(low), "tensor")
    residual = hidden_in + attn.astype(f32)
    rstd_two = lax.rsqrt(jnp.mean(residual * residual, axis=-1, keepdims=True) + epsilon)
    unit_two = residual * rstd_two
    normed_two = (unit_two * gain_two).astype(low)
    gate_pre = dot32(normed_two, gate_w)
    up_value = dot32(normed_two, up_w)
    sig = jax.nn.sigmoid(gate_pre)
    activation = (gate_pre * sig * up_value).astype(low)
    grad_low = grad_out.astype(low)
    d_activation = dot32(grad_low, down_w)
    d_gate_pre = (d_activation * up_value * sig * (1.0 + gate_pre * (1.0 - sig))).astype(low)
    d_up_value = (d_activation * gate_pre * sig).astype(low)
    dnormed_two = lax.psum(
        (dot32(d_gate_pre, gate_w, 1, 1) + dot32(d_up_value, up_w, 1, 1)).astype(low), "tensor"
    ).astype(f32)
    block_out = residual + lax.psum(
        dot32(activation, down_w, 1, 1).astype(low), "tensor"
    ).astype(f32)
    d_w_down = scatter(dot32(grad_low, activation, 0, 0).astype(low))
    d_w_gate = scatter(dot32(normed_two, d_gate_pre, 0, 0).astype(low))
    d_w_up = scatter(dot32(normed_two, d_up_value, 0, 0).astype(low))

    d_mlp_gain = jnp.sum(dnormed_two * unit_two, axis=0)
    d_residual = grad_out + norm_back(dnormed_two * gain_two, unit_two, rstd_two)
    residual_low = d_residual.astype(low)
    d_gated = dot32(residual_low, w_out)
    d_mixed, gate_low, gain_part, direct = call(
        functools.partial(gate_back_kernel, heads),
        [
            ((tokens, vw), low), ((tokens, vw), low), ((1, HEAD_V), f32),
            ((heads, HEAD_K, HEAD_V), f32),
        ],
        proj, mixed, d_gated, lifted, reading, gain_g,
    )
    directs = lax.all_gather(direct.astype(low), "context")
    dq, dk, dv, dg = call(
        functools.partial(intra_back_kernel, heads),
        [
            ((tokens, kw), f32), ((tokens, kw), f32), ((tokens, vw), f32), ((tokens, kw), f32),
        ],
        proj, total, d_mixed, seg_col, seg_row,
    )
    after = (order > here)[:, None, None]
    later = chain(
        jnp.where(after, passing, 1.0)[::-1],
        jnp.where(after[..., None], directs.astype(f32), 0.0)[::-1],
    )
    through = passing[here] * jnp.sum(prior * later, axis=-1)
    low_all, rank_out_part, bias_part = call(
        functools.partial(finish_kernel, heads, rank),
        [((tokens, wide), low), ((kw, rank), f32), ((1, kw), f32)],
        proj, total, d_mixed, lifted, reading, prior, later, through.reshape(1, kw), w_rank_out,
        bias, gate_low, dq, dk, dv, dg, seg_col, seg_row,
    )
    dnormed_one = lax.psum(dot32(low_all, w_in, 1, 1).astype(low), "tensor").astype(f32)
    d_w_in = scatter(
        jnp.concatenate(
            [dot32(normed_one, low_all, 0, 0).astype(low), dot32(residual_low, gated, 0, 0).astype(low)],
            axis=1,
        )
    ).astype(f32)
    d_norm_gain = jnp.sum(dnormed_one * unit_one, axis=0)
    d_block_in = d_residual + norm_back(dnormed_one * gain_one, unit_one, rstd_one)
    gains = scatter(jnp.stack([d_norm_gain, d_mlp_gain], axis=1))
    d_rank_in = lax.psum(d_w_in[:, base : base + rank], "tensor")
    small = lax.psum(
        jnp.concatenate([rank_out_part.reshape(-1), bias_part[0]]), ("dp", "context")
    )
    d_group = lax.psum(gain_part[0], ("dp", "context", "tensor"))
    return (
        block_out[None],
        d_block_in[None],
        gains[:, 0],
        d_w_in[:, :kw],
        d_w_in[:, kw : 2 * kw],
        d_w_in[:, 2 * kw : 2 * kw + vw],
        d_w_in[:, 2 * kw + vw : base],
        d_rank_in,
        small[: kw * rank].reshape(kw, rank),
        small[kw * rank :],
        d_group,
        d_w_in[:, wide:],
        gains[:, 1],
        d_w_gate.astype(f32),
        d_w_up.astype(f32),
        d_w_down.astype(f32),
    )


def solution(mesh):
    placed = (
        P("dp", "context", None),
        P("dp", "context"),
        P("dp", "context", None),
        P(("dp", "context")),
        P(("dp", "context"), "tensor"),
        P(("dp", "context"), "tensor"),
        P(("dp", "context"), "tensor"),
        P(("dp", "context"), "tensor"),
        P(("dp", "context"), None),
        P("tensor", None),
        P("tensor"),
        P(),
        P(("dp", "context"), "tensor"),
        P(("dp", "context")),
        P(("dp", "context"), "tensor"),
        P(("dp", "context"), "tensor"),
        P(("dp", "context"), "tensor"),
    )
    return jax.shard_map(
        per_device,
        mesh=mesh,
        in_specs=placed,
        out_specs=(
            P("dp", "context", None),
            P("dp", "context", None),
            P(("dp", "context")),
            P(("dp", "context"), "tensor"),
            P(("dp", "context"), "tensor"),
            P(("dp", "context"), "tensor"),
            P(("dp", "context"), "tensor"),
            P(("dp", "context"), None),
            P("tensor", None),
            P("tensor"),
            P(),
            P(("dp", "context"), "tensor"),
            P(("dp", "context")),
            P(("dp", "context"), "tensor"),
            P(("dp", "context"), "tensor"),
            P(("dp", "context"), "tensor"),
        ),
        check_vma=False,
    )
```

```python
import functools

import jax
import jax.numpy as jnp
from jax import lax
from jax.experimental import pallas as pl
from jax.experimental.pallas import tpu as pltpu
from jax.sharding import PartitionSpec as P

HEAD_K = 128
HEAD_V = 256
TILE = 256

epsilon = 1e-06
gate_divisor = 16.0
highest_precision = lax.Precision.HIGHEST
low = jnp.bfloat16
f32 = jnp.float32
MESH = pl.DeviceIdType.MESH
VMEM = pl.BlockSpec(memory_space=pltpu.VMEM)


def mm(a, b, ca=1, cb=0):
    return lax.dot_general(
        a.astype(low), b.astype(low), (((ca,), (cb,)), ((), ())), preferred_element_type=f32
    )


def mm_full(a, b, ca=1, cb=0):
    return lax.dot_general(
        a, b, (((ca,), (cb,)), ((), ())), precision=highest_precision, preferred_element_type=f32
    )


def mask_sum(mask, values):
    hi = values.astype(low)
    rest = values - hi.astype(f32)
    mid = rest.astype(low)
    last = (rest - mid.astype(f32)).astype(low)
    return mm(mask, hi) + mm(mask, mid) + mm(mask, last)


def level_factor(total, half):
    rows, width = total.shape
    if 2 * half >= 16:
        cube = total.reshape(rows // (2 * half), 2 * half, width)
        diff = cube - cube[:, half - 1 : half, :]
    else:
        cube = total.reshape(rows // 8, 8, width)
        sub = lax.broadcasted_iota(jnp.int32, cube.shape, 1)
        mid = cube[:, half - 1 : half, :]
        for block in range(1, 8 // (2 * half)):
            at = block * 2 * half
            mid = jnp.where(sub >= at, cube[:, at + half - 1 : at + half, :], mid)
        diff = cube - mid
    return jnp.exp(jnp.minimum(diff, -diff)).reshape(rows, width)


def small_levels(tile):
    half = tile // 2
    out = []
    while half >= 1:
        out.append(half)
        half //= 2
    return out


def level_mask(half, tile):
    t = lax.broadcasted_iota(jnp.int32, (tile, tile), 0)
    s = lax.broadcasted_iota(jnp.int32, (tile, tile), 1)
    return (t // (2 * half) == s // (2 * half)) & (t % (2 * half) >= half) & (s % (2 * half) < half)


def large_levels(rows, tile):
    half = rows // 2
    out = []
    while half >= tile:
        out.append(half)
        half //= 2
    return out


def local_kernel(heads, proj, rank_out, bias, seg_col, seg_row, out_ref, state_ref, lifted_ref, total_ref, tail_ref):
    rows = proj.shape[0]
    tile = min(TILE, rows)
    kw, vw = heads * HEAD_K, heads * HEAD_V
    rank = rank_out.shape[1]
    rank_act = proj[:, 2 * kw + 2 * vw : 2 * kw + 2 * vw + rank]
    decay = jax.nn.log_sigmoid(mm_full(rank_act, rank_out[...], 1, 1) + bias[...]) / gate_divisor
    segc, segr = seg_col[...], seg_row[...]
    t = lax.broadcasted_iota(jnp.int32, (rows, rows), 0)
    s = lax.broadcasted_iota(jnp.int32, (rows, rows), 1)
    total = mask_sum((t >= s).astype(low), decay)
    total_ref[...] = total
    same = segc == segr
    tail = (segc == segr[:, rows - 1 : rows]).astype(f32)
    for h in range(heads):
        q = proj[:, h * HEAD_K : (h + 1) * HEAD_K] * HEAD_K**-0.5
        k = proj[:, kw + h * HEAD_K : kw + (h + 1) * HEAD_K]
        v = proj[:, 2 * kw + h * HEAD_V : 2 * kw + (h + 1) * HEAD_V].astype(low)
        g = total[:, h * HEAD_K : (h + 1) * HEAD_K]
        diag = jnp.sum(q * k, axis=1, keepdims=True)
        ti = lax.broadcasted_iota(jnp.int32, (tile, tile), 0)
        si = lax.broadcasted_iota(jnp.int32, (tile, tile), 1)
        tiles = rows // tile
        sums = [
            jnp.where(ti == si, diag[i * tile : (i + 1) * tile], 0.0) for i in range(tiles)
        ]
        for half in small_levels(tile):
            factor = level_factor(g, half)
            qh, kh = (q * factor).astype(low), (k * factor).astype(low)
            mask = level_mask(half, tile)
            for i in range(tiles):
                span = slice(i * tile, (i + 1) * tile)
                sums[i] = jnp.where(mask, mm(qh[span], kh[span], 1, 1), sums[i])
        outs = []
        for i in range(tiles):
            span = slice(i * tile, (i + 1) * tile)
            sc = jnp.where(same[span, span] & (ti >= si), sums[i], 0.0)
            outs.append(mm(sc, v[span]))
        for half in large_levels(rows, tile):
            factor = level_factor(g, half)
            qh, kh = (q * factor).astype(low), (k * factor).astype(low)
            for at in range(0, rows, 2 * half):
                right, left = slice(at + half, at + 2 * half), slice(at, at + half)
                sc = jnp.where(same[right, left], mm(qh[right], kh[left], 1, 1), 0.0)
                more = mm(sc, v[left])
                for i in range(half // tile):
                    outs[(at + half) // tile + i] += more[i * tile : (i + 1) * tile]
        for i in range(tiles):
            out_ref[i * tile : (i + 1) * tile, h * HEAD_V : (h + 1) * HEAD_V] = outs[i]
        end = g[rows - 1 : rows]
        kt = k * jnp.exp(end - g) * tail
        state_ref[h] = mm(kt, v, 0, 0)
        lifted_ref[:, h * HEAD_K : (h + 1) * HEAD_K] = (q * jnp.exp(g)).astype(low)
        tail_ref[:, h * HEAD_K : (h + 1) * HEAD_K] = jnp.exp(end)


def intra_back_kernel(heads, proj, total_in, d_mixed, seg_col, seg_row, dq_ref, dk_ref, dv_ref, dg_ref):
    rows = proj.shape[0]
    tile = min(TILE, rows)
    tiles = rows // tile
    kw = heads * HEAD_K
    same = seg_col[...] == seg_row[...]
    ti = lax.broadcasted_iota(jnp.int32, (tile, tile), 0)
    si = lax.broadcasted_iota(jnp.int32, (tile, tile), 1)
    for h in range(heads):
        cols = slice(h * HEAD_K, (h + 1) * HEAD_K)
        vcols = slice(h * HEAD_V, (h + 1) * HEAD_V)
        q = proj[:, cols] * HEAD_K**-0.5
        k = proj[:, kw + h * HEAD_K : kw + (h + 1) * HEAD_K]
        v = proj[:, 2 * kw + h * HEAD_V : 2 * kw + (h + 1) * HEAD_V].astype(low)
        do = d_mixed[:, vcols].astype(low)
        g = total_in[:, cols]
        diag = jnp.sum(q * k, axis=1, keepdims=True)
        d_diag = jnp.sum(do.astype(f32) * v.astype(f32), axis=1, keepdims=True)
        sums = [jnp.where(ti == si, diag[i * tile : (i + 1) * tile], 0.0) for i in range(tiles)]
        allowed = [same[i * tile : (i + 1) * tile, i * tile : (i + 1) * tile] for i in range(tiles)]
        ds = [
            jnp.where(
                allowed[i],
                mm(do[i * tile : (i + 1) * tile], v[i * tile : (i + 1) * tile], 1, 1),
                0.0,
            ).astype(low)
            for i in range(tiles)
        ]
        dq = [(d_diag * k)[i * tile : (i + 1) * tile] for i in range(tiles)]
        dk = [(d_diag * q)[i * tile : (i + 1) * tile] for i in range(tiles)]
        dg = [jnp.zeros((tile, HEAD_K), f32) for i in range(tiles)]
        for half in small_levels(tile):
            factor = level_factor(g, half)
            qh, kh = (q * factor).astype(low), (k * factor).astype(low)
            mask = level_mask(half, tile)
            for i in range(tiles):
                span = slice(i * tile, (i + 1) * tile)
                sums[i] = jnp.where(mask, mm(qh[span], kh[span], 1, 1), sums[i])
                part = jnp.where(mask, ds[i], jnp.zeros((), low))
                dql = mm(part, kh[span])
                dkl = mm(part, qh[span], 0, 0)
                dq[i] += dql * factor[span]
                dk[i] += dkl * factor[span]
                dg[i] += qh[span].astype(f32) * dql - kh[span].astype(f32) * dkl
        dv = []
        for i in range(tiles):
            span = slice(i * tile, (i + 1) * tile)
            sc = jnp.where(allowed[i] & (ti >= si), sums[i], 0.0)
            dv.append(mm(sc, do[span], 0, 0))
        for half in large_levels(rows, tile):
            factor = level_factor(g, half)
            qh, kh = (q * factor).astype(low), (k * factor).astype(low)
            for at in range(0, rows, 2 * half):
                right, left = slice(at + half, at + 2 * half), slice(at, at + half)
                ok = same[right, left]
                sc = jnp.where(ok, mm(qh[right], kh[left], 1, 1), 0.0)
                part = jnp.where(ok, mm(do[right], v[left], 1, 1), 0.0).astype(low)
                dvl = mm(sc, do[right], 0, 0)
                dql = mm(part, kh[left])
                dkl = mm(part, qh[right], 0, 0)
                dgr = qh[right].astype(f32) * dql
                dgl = kh[left].astype(f32) * dkl
                dql = dql * factor[right]
                dkl = dkl * factor[left]
                for i in range(half // tile):
                    piece = slice(i * tile, (i + 1) * tile)
                    r, l = (at + half) // tile + i, at // tile + i
                    dq[r] += dql[piece]
                    dg[r] += dgr[piece]
                    dk[l] += dkl[piece]
                    dg[l] -= dgl[piece]
                    dv[l] += dvl[piece]
        for i in range(tiles):
            span = slice(i * tile, (i + 1) * tile)
            dq_ref[span, cols] = dq[i]
            dk_ref[span, cols] = dk[i]
            dg_ref[span, cols] = dg[i]
            dv_ref[span, vcols] = dv[i]


def silu_parts(gate):
    sig = jax.nn.sigmoid(gate)
    return sig, gate * sig


def mix_kernel(heads, proj, out_local, lifted, reading, prior, gain, mixed_ref, gated_ref):
    kw, vw = heads * HEAD_K, heads * HEAD_V
    for h in range(heads):
        vcols = slice(h * HEAD_V, (h + 1) * HEAD_V)
        mixed = out_local[:, vcols] + reading[...] * mm(
            lifted[:, h * HEAD_K : (h + 1) * HEAD_K], prior[h]
        )
        mixed_ref[:, vcols] = mixed
        rms = lax.rsqrt(jnp.mean(mixed * mixed, axis=1, keepdims=True) + epsilon)
        gate = proj[:, 2 * kw + vw + h * HEAD_V : 2 * kw + vw + (h + 1) * HEAD_V]
        gated_ref[:, vcols] = (mixed * rms * gain[...] * silu_parts(gate)[1]).astype(low)


def gate_back_kernel(heads, proj, mixed_in, d_gated_in, lifted, reading, gain, d_mixed_ref, gate_low_ref, gain_ref, direct_ref):
    kw, vw = heads * HEAD_K, heads * HEAD_V
    gain_sum = jnp.zeros((1, HEAD_V), f32)
    for h in range(heads):
        vcols = slice(h * HEAD_V, (h + 1) * HEAD_V)
        mixed = mixed_in[:, vcols]
        dy = d_gated_in[:, vcols]
        gate = proj[:, 2 * kw + vw + h * HEAD_V : 2 * kw + vw + (h + 1) * HEAD_V]
        sig, act = silu_parts(gate)
        rms = lax.rsqrt(jnp.mean(mixed * mixed, axis=1, keepdims=True) + epsilon)
        unit = mixed * rms
        gate_low_ref[:, vcols] = (
            dy * unit * gain[...] * sig * (1.0 + gate * (1.0 - sig))
        ).astype(low)
        gain_sum += jnp.sum(dy * act * unit, axis=0, keepdims=True)
        e = dy * act * gain[...]
        d_mixed = rms * (e - unit * jnp.mean(e * unit, axis=1, keepdims=True))
        d_mixed = d_mixed.astype(low)
        d_mixed_ref[:, vcols] = d_mixed
        read = lifted[:, h * HEAD_K : (h + 1) * HEAD_K] * reading[...].astype(low)
        direct_ref[h] = mm(read, d_mixed, 0, 0)
    gain_ref[...] = gain_sum


def finish_kernel(heads, rank, proj, total_in, d_mixed, lifted, reading, prior, later, through, rank_out, bias, gate_low, dq_in, dk_in, dv_in, dg_in, seg_col, seg_row, low_ref, rank_out_ref, bias_ref):
    rows = proj.shape[0]
    kw, vw = heads * HEAD_K, heads * HEAD_V
    segc, segr = seg_col[...], seg_row[...]
    t = lax.broadcasted_iota(jnp.int32, (rows, rows), 0)
    s = lax.broadcasted_iota(jnp.int32, (rows, rows), 1)
    suffix = ((t <= s) & (segc == segr)).astype(low)
    tail = (segc == segr[:, rows - 1 : rows]).astype(f32)
    read = reading[...]
    base = 2 * kw + 2 * vw
    rank_act = proj[:, base : base + rank]
    pre = mm_full(rank_act, rank_out[...], 1, 1) + bias[...]
    rank_part = jnp.zeros((rows, rank), f32)
    for h in range(heads):
        cols = slice(h * HEAD_K, (h + 1) * HEAD_K)
        vcols = slice(h * HEAD_V, (h + 1) * HEAD_V)
        k = proj[:, kw + h * HEAD_K : kw + (h + 1) * HEAD_K]
        v = proj[:, 2 * kw + h * HEAD_V : 2 * kw + (h + 1) * HEAD_V].astype(low)
        do = d_mixed[:, vcols]
        g = total_in[:, cols]
        end = g[rows - 1 : rows]
        pulled = mm(do, prior[h], 1, 1) * read
        dq = dq_in[:, cols] + pulled * jnp.exp(g)
        fall = jnp.exp(end - g) * tail
        kt = (k * fall).astype(low)
        dkt = mm(v, later[h], 1, 1)
        dk = dk_in[:, cols] + dkt * fall
        crossing = kt.astype(f32) * dkt
        dv = dv_in[:, vcols] + mm(kt, later[h])
        dg = dg_in[:, cols] + pulled * lifted[:, cols].astype(f32) - crossing
        across = jnp.sum(crossing, axis=0, keepdims=True) + through[:, cols]
        d_decay = mask_sum(suffix, dg) + tail * across
        d_pre = d_decay * jax.nn.sigmoid(-pre[:, cols]) / gate_divisor
        low_ref[:, cols] = (dq * HEAD_K**-0.5).astype(low)
        low_ref[:, kw + h * HEAD_K : kw + (h + 1) * HEAD_K] = dk.astype(low)
        low_ref[:, 2 * kw + h * HEAD_V : 2 * kw + (h + 1) * HEAD_V] = dv.astype(low)
        rank_part += mm_full(d_pre, rank_out[cols, :])
        rank_out_ref[cols, :] = mm_full(d_pre, rank_act, 0, 0)
        bias_ref[:, cols] = jnp.sum(d_pre, axis=0, keepdims=True)
    low_ref[:, 2 * kw + vw : base] = gate_low[...]
    wide = low_ref.shape[1] - base
    low_ref[:, base:] = jnp.concatenate(
        [rank_part, jnp.zeros((rows, wide - rank), f32)], axis=1
    ).astype(low)


def call(kernel, outs, *args):
    return pl.pallas_call(
        kernel,
        out_shape=[jax.ShapeDtypeStruct(shape, kind) for shape, kind in outs],
        in_specs=[VMEM] * len(args),
        out_specs=[VMEM] * len(outs),
        compiler_params=pltpu.CompilerParams(vmem_limit_bytes=56 * 1024 * 1024),
    )(*args)


def sum_kernel(n, x_ref, out_ref, arrived, total, send_sem, recv_sem, back_send, back_recv):
    me = lax.axis_index("tensor")
    rows = x_ref.shape[0] // n
    barrier = pltpu.get_barrier_semaphore()
    for d in range(1, n):
        pl.semaphore_signal(
            barrier, inc=1, device_id={"tensor": lax.rem(me + d, n)}, device_id_type=MESH
        )
    pl.semaphore_wait(barrier, n - 1)
    sends = []
    for d in range(1, n):
        peer = lax.rem(me + d, n)
        copy = pltpu.make_async_remote_copy(
            src_ref=x_ref.at[pl.ds(pl.multiple_of(peer * rows, rows), rows)],
            dst_ref=arrived.at[d - 1],
            send_sem=send_sem.at[d - 1],
            recv_sem=recv_sem.at[d - 1],
            device_id={"tensor": peer},
            device_id_type=MESH,
        )
        copy.start()
        sends.append(copy)
    mine = pl.ds(pl.multiple_of(me * rows, rows), rows)
    value = x_ref[mine, :].astype(f32)
    for d in range(1, n):
        sends[d - 1].wait_recv()
        value = value + arrived[d - 1].astype(f32)
    total[...] = value.astype(low)
    backs = []
    for d in range(1, n):
        copy = pltpu.make_async_remote_copy(
            src_ref=total,
            dst_ref=out_ref.at[mine],
            send_sem=back_send.at[d - 1],
            recv_sem=back_recv.at[d - 1],
            device_id={"tensor": lax.rem(me + d, n)},
            device_id_type=MESH,
        )
        copy.start()
        backs.append(copy)
    out_ref[mine, :] = value.astype(low)
    for d in range(1, n):
        sends[d - 1].wait_send()
        backs[d - 1].wait()


def tensor_sum(x):
    n = lax.axis_size("tensor")
    rows = x.shape[0] // n
    return pl.pallas_call(
        functools.partial(sum_kernel, n),
        out_shape=jax.ShapeDtypeStruct(x.shape, x.dtype),
        in_specs=[VMEM],
        out_specs=VMEM,
        scratch_shapes=[
            pltpu.VMEM((n - 1, rows, x.shape[1]), x.dtype),
            pltpu.VMEM((rows, x.shape[1]), x.dtype),
            pltpu.SemaphoreType.DMA((n - 1,)),
            pltpu.SemaphoreType.DMA((n - 1,)),
            pltpu.SemaphoreType.DMA((n - 1,)),
            pltpu.SemaphoreType.DMA((n - 1,)),
        ],
        compiler_params=pltpu.CompilerParams(
            collective_id=0, has_side_effects=True, vmem_limit_bytes=32 * 1024 * 1024
        ),
    )(x)


def norm_back(scaled_grad, unit_rows, rstd_rows):
    return rstd_rows * (
        scaled_grad - unit_rows * jnp.mean(scaled_grad * unit_rows, axis=-1, keepdims=True)
    )


def gather(value):
    return lax.all_gather(value, ("dp", "context"), axis=0, tiled=True)


def scatter(value):
    for axis in ("dp", "context"):
        value = lax.psum_scatter(value, axis, scatter_dimension=0, tiled=True)
    return value


def dot32(a, b, ca=1, cb=0):
    return lax.dot_general(a, b, (((ca,), (cb,)), ((), ())), preferred_element_type=f32)


def chain(factors, values):
    weight = jnp.ones_like(factors[0])
    out = jnp.zeros_like(values[0])
    for j in reversed(range(factors.shape[0])):
        out = out + weight[..., None] * values[j]
        weight = weight * factors[j]
    return out


def per_device(
    block_in, segments, cotangent, norm_gain, w_query, w_key, w_value, w_gate_out, w_rank_in,
    w_rank_out, gate_bias, group_gain, w_output, mlp_gain, w_gate, w_up, w_down,
):
    hidden_in, seg, grad_out = block_in[0], segments[0], cotangent[0]
    tokens, width = hidden_in.shape
    rank = w_rank_in.shape[1]
    heads = w_rank_out.shape[0] // HEAD_K
    kw, vw = heads * HEAD_K, heads * HEAD_V
    base = 2 * kw + 2 * vw
    rest = -(rank + 2) % 128 + rank + 2
    rows_here = w_query.shape[0]
    seg_col, seg_row = seg[:, None], seg[None, :]
    bias = gate_bias[None, :]
    gain_g = group_gain[None, :]

    packed = jnp.concatenate(
        [
            w_query, w_key, w_value, w_gate_out, w_rank_in, norm_gain[:, None], mlp_gain[:, None],
            jnp.zeros((rows_here, rest - rank - 2), low), w_output,
        ],
        axis=1,
    )
    mixer = gather(packed)
    hidden = w_gate.shape[1]
    mlp = gather(jnp.concatenate([w_gate, w_up, w_down], axis=1))
    gate_w, up_w, down_w = mlp[:, :hidden], mlp[:, hidden : 2 * hidden], mlp[:, 2 * hidden :]
    wide = base + rest
    w_in = mixer[:, :wide]
    w_out = mixer[:, wide:]
    gain_one = mixer[:, base + rank].astype(f32)
    gain_two = mixer[:, base + rank + 1].astype(f32)

    rstd_one = lax.rsqrt(jnp.mean(hidden_in * hidden_in, axis=-1, keepdims=True) + epsilon)
    unit_one = hidden_in * rstd_one
    normed_one = (unit_one * gain_one).astype(low)
    proj = dot32(normed_one, w_in)
    out_local, state_local, lifted, total, ends = call(
        functools.partial(local_kernel, heads),
        [
            ((tokens, vw), f32), ((heads, HEAD_K, HEAD_V), f32), ((tokens, kw), low),
            ((tokens, kw), f32), ((1, kw), f32),
        ],
        proj, w_rank_out, bias, seg_col, seg_row,
    )
    peers, here = lax.axis_size("context"), lax.axis_index("context")
    firsts = lax.all_gather(jnp.stack([seg[0], seg[-1]]).astype(f32), "context")
    states = lax.all_gather(
        jnp.concatenate(
            [
                state_local.reshape(kw, HEAD_V),
                jnp.broadcast_to(ends.reshape(kw, 1), (kw, 128)),
            ],
            axis=1,
        ),
        "context",
    )
    order = jnp.arange(peers)
    first, last = firsts[:, 0], firsts[:, 1]
    before = jnp.concatenate([jnp.full((1,), -1.0, f32), last[:-1]])
    keep = jnp.where((first == before) | (before < 0.0), 1.0, 0.0)
    unbroken = jnp.where(first == last, 1.0, 0.0)
    decays = states[:, :, HEAD_V].reshape(peers, heads, HEAD_K)
    spans = decays * unbroken[:, None, None]
    passing = spans * keep[:, None, None]
    earlier = (order < here)[:, None, None]
    prior = chain(
        jnp.where(earlier, passing, 1.0),
        jnp.where(earlier[..., None], states[:, :, :HEAD_V].reshape(peers, heads, HEAD_K, HEAD_V), 0.0),
    )
    prior_last = jnp.where(here > 0, before[here], -1.0)
    reading = (seg.astype(f32) == prior_last).astype(f32)[:, None]

    mixed, gated = call(
        functools.partial(mix_kernel, heads),
        [((tokens, vw), f32), ((tokens, vw), low)],
        proj, out_local, lifted, reading, prior, gain_g,
    )
    attn = tensor_sum(dot32(gated, w_out, 1, 1).astype(low))
    residual = hidden_in + attn.astype(f32)
    rstd_two = lax.rsqrt(jnp.mean(residual * residual, axis=-1, keepdims=True) + epsilon)
    unit_two = residual * rstd_two
    normed_two = (unit_two * gain_two).astype(low)
    gate_pre = dot32(normed_two, gate_w)
    up_value = dot32(normed_two, up_w)
    sig = jax.nn.sigmoid(gate_pre)
    activation = (gate_pre * sig * up_value).astype(low)
    grad_low = grad_out.astype(low)
    d_activation = dot32(grad_low, down_w)
    d_gate_pre = (d_activation * up_value * sig * (1.0 + gate_pre * (1.0 - sig))).astype(low)
    d_up_value = (d_activation * gate_pre * sig).astype(low)
    dnormed_two = tensor_sum(
        (dot32(d_gate_pre, gate_w, 1, 1) + dot32(d_up_value, up_w, 1, 1)).astype(low)
    ).astype(f32)
    mlp_part = dot32(activation, down_w, 1, 1).astype(low)
    d_mlp = scatter(
        jnp.concatenate(
            [
                dot32(normed_two, d_gate_pre, 0, 0).astype(low),
                dot32(normed_two, d_up_value, 0, 0).astype(low),
                dot32(grad_low, activation, 0, 0).astype(low),
            ],
            axis=1,
        )
    ).astype(f32)

    d_mlp_gain = jnp.sum(dnormed_two * unit_two, axis=0)
    d_residual = grad_out + norm_back(dnormed_two * gain_two, unit_two, rstd_two)
    residual_low = d_residual.astype(low)
    d_gated = dot32(residual_low, w_out)
    d_mixed, gate_low, gain_part, direct = call(
        functools.partial(gate_back_kernel, heads),
        [
            ((tokens, vw), low), ((tokens, vw), low), ((1, HEAD_V), f32),
            ((heads, HEAD_K, HEAD_V), f32),
        ],
        proj, mixed, d_gated, lifted, reading, gain_g,
    )
    directs = lax.all_gather(direct.astype(low), "context")
    dq, dk, dv, dg = call(
        functools.partial(intra_back_kernel, heads),
        [
            ((tokens, kw), f32), ((tokens, kw), f32), ((tokens, vw), f32), ((tokens, kw), f32),
        ],
        proj, total, d_mixed, seg_col, seg_row,
    )
    after = (order > here)[:, None, None]
    later = chain(
        jnp.where(after, passing, 1.0)[::-1],
        jnp.where(after[..., None], directs.astype(f32), 0.0)[::-1],
    )
    through = passing[here] * jnp.sum(prior * later, axis=-1)
    low_all, rank_out_part, bias_part = call(
        functools.partial(finish_kernel, heads, rank),
        [((tokens, wide), low), ((kw, rank), f32), ((1, kw), f32)],
        proj, total, d_mixed, lifted, reading, prior, later, through.reshape(1, kw), w_rank_out,
        bias, gate_low, dq, dk, dv, dg, seg_col, seg_row,
    )
    dnormed_one = tensor_sum(dot32(low_all, w_in, 1, 1).astype(low))
    d_w_in = scatter(
        jnp.concatenate(
            [dot32(normed_one, low_all, 0, 0).astype(low), dot32(residual_low, gated, 0, 0).astype(low)],
            axis=1,
        )
    ).astype(f32)
    mlp_part, dnormed_one = lax.optimization_barrier((mlp_part, dnormed_one))
    dnormed_one = dnormed_one.astype(f32)
    block_out = residual + tensor_sum(mlp_part).astype(f32)
    d_norm_gain = jnp.sum(dnormed_one * unit_one, axis=0)
    d_block_in = d_residual + norm_back(dnormed_one * gain_one, unit_one, rstd_one)
    index = lax.axis_index("dp") * peers + here
    width_here = norm_gain.shape[0]
    gains = lax.psum(jnp.stack([d_norm_gain, d_mlp_gain]), ("dp", "context"))
    gains = lax.dynamic_slice_in_dim(gains, index * width_here, width_here, axis=1)
    small = lax.psum(
        jnp.concatenate([rank_out_part.reshape(-1), bias_part[0], gain_part[0]]),
        ("dp", "context"),
    )
    d_rank_in = d_w_in[:, base : base + rank]
    across = lax.psum(
        jnp.concatenate([d_rank_in.reshape(-1), small[kw * (rank + 1) :]]), "tensor"
    )
    d_rank_in = across[: d_rank_in.size].reshape(d_rank_in.shape)
    d_group = across[d_rank_in.size :]
    return (
        block_out[None],
        d_block_in[None],
        gains[0],
        d_w_in[:, :kw],
        d_w_in[:, kw : 2 * kw],
        d_w_in[:, 2 * kw : 2 * kw + vw],
        d_w_in[:, 2 * kw + vw : base],
        d_rank_in,
        small[: kw * rank].reshape(kw, rank),
        small[kw * rank : kw * (rank + 1)],
        d_group,
        d_w_in[:, wide:],
        gains[1],
        d_mlp[:, :hidden],
        d_mlp[:, hidden : 2 * hidden],
        d_mlp[:, 2 * hidden :],
    )


def solution(mesh):
    placed = (
        P("dp", "context", None),
        P("dp", "context"),
        P("dp", "context", None),
        P(("dp", "context")),
        P(("dp", "context"), "tensor"),
        P(("dp", "context"), "tensor"),
        P(("dp", "context"), "tensor"),
        P(("dp", "context"), "tensor"),
        P(("dp", "context"), None),
        P("tensor", None),
        P("tensor"),
        P(),
        P(("dp", "context"), "tensor"),
        P(("dp", "context")),
        P(("dp", "context"), "tensor"),
        P(("dp", "context"), "tensor"),
        P(("dp", "context"), "tensor"),
    )
    return jax.shard_map(
        per_device,
        mesh=mesh,
        in_specs=placed,
        out_specs=(
            P("dp", "context", None),
            P("dp", "context", None),
            P(("dp", "context")),
            P(("dp", "context"), "tensor"),
            P(("dp", "context"), "tensor"),
            P(("dp", "context"), "tensor"),
            P(("dp", "context"), "tensor"),
            P(("dp", "context"), None),
            P("tensor", None),
            P("tensor"),
            P(),
            P(("dp", "context"), "tensor"),
            P(("dp", "context")),
            P(("dp", "context"), "tensor"),
            P(("dp", "context"), "tensor"),
            P(("dp", "context"), "tensor"),
        ),
        check_vma=False,
    )
```
